32 devices in a mesh: dp: 16 (over z, y, core), tensor: 2 (over x).
Axes of the slice: x: 2, y: 2, z: 4, core: 2. Of those that a mesh axis runs over, the one named last changes fastest.
Arguments:
- residual_in: float32 [8192, 1024], P(('dp', 'tensor')), may hold values from -6 to 6
- out_cotangent: float32 [8192, 1024], P(('dp', 'tensor')), may hold values from -6 to 6
- seq_lengths: int32 [4], replicated, may hold values from 1 to 4096, 8192 in all
- qkv_weight: float32 [1024, 3072], P('dp', 'tensor'), may hold values from -1 to 1
- out_weight: float32 [1024, 1024], P('tensor', 'dp'), may hold values from -2 to 2
- in_weight: float32 [1024, 2, 2624], P('dp', None, 'tensor'), may hold values from -0.1875 to 0.1875
- down_weight: float32 [2624, 1024], P('tensor', 'dp'), may hold values from -0.125 to 0.125
- norm_gains: float32 [2, 1024], replicated, may hold values from 0.5 to 1.5
- qkv_moments: float32 [2, 1024, 3072], P(None, 'dp', 'tensor'), may hold values from -8192 to 8192, as said below
- out_moments: float32 [2, 1024, 1024], P(None, 'tensor', 'dp'), may hold values from -8192 to 8192, as said below
- in_moments: float32 [2, 1024, 2, 2624], P(None, 'dp', None, 'tensor'), may hold values from -8192 to 8192, as said below
- down_moments: float32 [2, 2624, 1024], P(None, 'tensor', 'dp'), may hold values from -8192 to 8192, as said below
- gain_moments: float32 [2, 2, 1024], replicated, may hold values from -8192 to 8192, as said below
Outputs:
- block_out: float32 [8192, 1024], P(('dp', 'tensor'))
- residual_grad: float32 [8192, 1024], P(('dp', 'tensor'))
- qkv_grad: float32 [1024, 3072], P('dp', 'tensor')
- out_weight_grad: float32 [1024, 1024], P('tensor', 'dp')
- in_grad: float32 [1024, 2, 2624], P('dp', None, 'tensor')
- down_grad: float32 [2624, 1024], P('tensor', 'dp')
- gains_grad: float32 [2, 1024], replicated
- new_qkv: float32 [1024, 3072], P('dp', 'tensor')
- new_out: float32 [1024, 1024], P('tensor', 'dp')
- new_in: float32 [1024, 2, 2624], P('dp', None, 'tensor')
- new_down: float32 [2624, 1024], P('tensor', 'dp')
- new_gains: float32 [2, 1024], replicated
- new_qkv_moments: float32 [2, 1024, 3072], P(None, 'dp', 'tensor')
- new_out_moments: float32 [2, 1024, 1024], P(None, 'tensor', 'dp')
- new_in_moments: float32 [2, 1024, 2, 2624], P(None, 'dp', None, 'tensor')
- new_down_moments: float32 [2, 2624, 1024], P(None, 'tensor', 'dp')
- new_gain_moments: float32 [2, 2, 1024], replicated
The draws below stay inside these ranges and needn't reach their ends.
Inputs may be any that keep to these rules, and one draw needn't show every extreme that they name: `seq_lengths`: the lengths sum to 8192; the longest is exactly 4096. `qkv_moments`: index 0 is the first moment, index 1 the second moment, which is positive. `out_moments`: index 0 is the first moment, index 1 the second moment, which is positive. `in_moments`: index 0 is the first moment, index 1 the second moment, which is positive. `down_moments`: index 0 is the first moment, index 1 the second moment, which is positive. `gain_moments`: index 0 is the first moment, index 1 the second moment, which is positive.
All inputs are finite; a program needn't handle non-finite values.
Results may differ from the reference program's by a relative error of at most 0.019.
Values may be sent and summed in bfloat16 or wider, within the bound.
A program may use at most 128 MiB of HBM per device.

```python
import math
import jax
import jax.numpy as jnp
import numpy as np
from jax import lax

D = 1024
H = 16
HD = 64
FF = 2624
HALF_WIN = 64
TOK_DEV = 512
NSEQ = 4
STEP = 3
TOKENS = 8192


def draw_qkv_weight(key, part):
    base_key = jax.random.fold_in(key, 11)
    draws = jax.random.normal(base_key, (D, 3 * D), jnp.float32) / math.sqrt(D)
    return jnp.clip(draws, -1.0, 1.0)


def moment_pair(key, salt, shape, grad_scale):
    first_key, second_key = jax.random.split(jax.random.fold_in(key, salt))
    first_moment = jnp.clip(0.13 * jax.random.normal(first_key, shape, jnp.float32), -0.6, 0.6) * grad_scale
    spread = jnp.exp(jax.random.uniform(second_key, shape, jnp.float32, math.log(0.2), math.log(20.0)))
    second_moment = 0.001 * grad_scale * grad_scale * spread
    return jnp.stack([first_moment, second_moment])


def draw_qkv_moments(key, part):
    return moment_pair(key, 31, (D, 3 * D), 2.0 * math.sqrt(TOKENS))


def draw_out_moments(key, part):
    return moment_pair(key, 37, (D, D), 0.2 * math.sqrt(TOKENS))


def draw_in_moments(key, part):
    return moment_pair(key, 41, (D, 2, FF), 0.4 * math.sqrt(TOKENS))


def draw_down_moments(key, part):
    return moment_pair(key, 43, (FF, D), 0.65 * math.sqrt(TOKENS))


def draw_gain_moments(key, part):
    row_scale = jnp.array([[4.0], [1.5]], jnp.float32) * math.sqrt(TOKENS)
    return moment_pair(key, 47, (2, D), row_scale)


def level_of(key, extent, cuts, smallest, high):
    def one(position, blocks):
        heights = jax.random.uniform(jax.random.fold_in(jax.random.fold_in(key, 6), position), (blocks,), jnp.float32, smallest / len(cuts), high / len(cuts))
        return jnp.repeat(jnp.exp(heights), extent[position] // blocks).reshape((-1,) + (1,) * (len(extent) - position - 1))

    level = one(*cuts[0])
    for cut in cuts[1:]:
        level = level * one(*cut)
    return level


def length_profile(amount, total, bound, skew):
    weights = [(1 << 20) // math.isqrt(grade ** skew) + 1 for grade in range(2, amount + 1)]
    spare, given = total - bound - (amount - 1), [1] * (amount - 1)
    while spare > 0:
        movable = [i for i in range(amount - 1) if given[i] < bound]
        whole, budget = sum([weights[i] for i in movable]), spare
        for i in movable:
            extra = min(bound - given[i], max(1, budget * weights[i] // whole), spare)
            given[i] = given[i] + extra
            spare = spare - extra
    return np.array([bound] + given)


def uneven_parts(own_key, amount, total, most, skew):
    if amount == 2:
        one = jax.random.randint(own_key, (), max(1, total - most), min(most, total - 1) + 1)
        return jnp.stack([one, total - one])
    tallies = jnp.asarray(length_profile(amount, total, most, skew), jnp.int32)
    couples = (amount - 1) // 2
    giver, taker = tallies[1:1 + 2 * couples:2], tallies[2:2 + 2 * couples:2]
    slack = jnp.minimum(giver - 1, most - taker)
    shifted = jax.random.randint(jax.random.fold_in(own_key, 1), (couples,), 0, 1 << 20) % (slack + 1)
    tallies = tallies.at[1:1 + 2 * couples:2].set(giver - shifted).at[2:2 + 2 * couples:2].set(taker + shifted)
    return tallies[jax.random.permutation(jax.random.fold_in(own_key, 2), amount)]


def bell_draw(stream_key, dims, deviation, most, cuts=(), kind=jnp.bfloat16):
    factor_of = level_of(stream_key, dims, cuts, -0.22, 0.18) if cuts else 1.0
    result = jax.random.normal(stream_key, dims, jnp.float32) * deviation * factor_of
    return jnp.minimum(jnp.maximum(result, -most), most).astype(kind)


def setup_inputs(seed: int = 0) -> dict:
    streams_of = jax.random.split(jax.random.key(seed), 14)
    return {
        "residual_in": bell_draw(streams_of[0], (TOKENS, D), 1.0, 6.0, ((0, 32),), jnp.float32),
        "out_cotangent": bell_draw(streams_of[1], (TOKENS, D), 1.0, 6.0, ((0, 32),), jnp.float32),
        "seq_lengths": uneven_parts(streams_of[2], NSEQ, TOKENS, TOKENS // 2, 2).astype(jnp.int32),
        "qkv_weight": draw_qkv_weight(jax.random.fold_in(streams_of[13], 71), 0),
        "out_weight": bell_draw(streams_of[4], (D, D), (max(D // (2 * HALF_WIN + 1), 1)) ** -0.5, 2.0, ((0, 2), (1, 16)), jnp.float32),
        "in_weight": bell_draw(streams_of[5], (D, 2, FF), D ** -0.5, 0.1875, ((0, 16), (2, 2)), jnp.float32),
        "down_weight": bell_draw(streams_of[6], (FF, D), FF ** -0.5, 0.125, ((0, 2), (1, 16)), jnp.float32),
        "norm_gains": jnp.clip(1.0 + 0.1 * jax.random.normal(streams_of[7], (2, D), jnp.float32), 0.5, 1.5),
        "qkv_moments": draw_qkv_moments(jax.random.fold_in(streams_of[13], 71), 0),
        "out_moments": draw_out_moments(jax.random.fold_in(streams_of[13], 71), 0),
        "in_moments": draw_in_moments(jax.random.fold_in(streams_of[13], 71), 0),
        "down_moments": draw_down_moments(jax.random.fold_in(streams_of[13], 71), 0),
        "gain_moments": draw_gain_moments(jax.random.fold_in(streams_of[13], 71), 0),
    }


NORM_EPS = 1e-05
ROPE_BASE = 10000.0
BETA_ONE = 0.9
BETA_TWO = 0.999
ADAM_EPS = 1e-08
LEARN_RATE = 0.005
DECAY_RATE = 0.1
MASKED = -1e+30

def to_bf16(array):
    return lax.optimization_barrier(array.astype(jnp.bfloat16))

def widen(array):
    return array.astype(jnp.float32)

def matmul(left, right):
    return jnp.dot(left, right, preferred_element_type=jnp.float32)

def norm_forward(rows, gain):
    row_mean = lax.optimization_barrier(jnp.mean(rows, axis=-1, keepdims=True))
    centered = rows - row_mean
    inv_std = lax.rsqrt(lax.optimization_barrier(jnp.mean(centered * centered, axis=-1, keepdims=True)) + NORM_EPS)
    normed = centered * inv_std
    return (normed, inv_std, normed * gain)

def norm_backward(grad_out, normed, inv_std, gain):
    scaled = grad_out * gain
    grad_rows = inv_std * (scaled - lax.optimization_barrier(jnp.mean(scaled, axis=-1, keepdims=True)) - normed * lax.optimization_barrier(jnp.mean(scaled * normed, axis=-1, keepdims=True)))
    return (grad_rows, lax.optimization_barrier(jnp.sum(grad_out * normed, axis=0)))

def seq_coords(seq_lengths, places):
    seq_ends = jnp.cumsum(seq_lengths, dtype=jnp.int32)
    passed = (seq_ends[None, :] <= places[:, None]).astype(jnp.int32)
    seq_ids = lax.optimization_barrier(jnp.sum(passed, axis=1, dtype=jnp.int32))
    seq_start = lax.optimization_barrier(jnp.sum(passed * seq_lengths[None, :], axis=1, dtype=jnp.int32))
    return (seq_ids, places - seq_start)

def rotary_tables(offsets, head_dim):
    half_dim = head_dim // 2
    inv_freq = ROPE_BASE ** (-2.0 * jnp.arange(half_dim).astype(jnp.float32) / head_dim)
    angles = offsets.astype(jnp.float32)[:, None] * inv_freq[None, :]
    cos_table = jnp.cos(angles)
    sin_table = jnp.sin(angles)
    return (jnp.concatenate([cos_table, cos_table], axis=-1), jnp.concatenate([sin_table, sin_table], axis=-1))

def rotate(feats, cos_table, sin_table):
    half_dim = feats.shape[-1] // 2
    turned = jnp.concatenate([-feats[..., half_dim:], feats[..., :half_dim]], axis=-1)
    return feats * cos_table[:, None, :] + turned * sin_table[:, None, :]

def unrotate(grads, cos_table, sin_table):
    half_dim = grads.shape[-1] // 2
    spun = grads * sin_table[:, None, :]
    back = jnp.concatenate([spun[..., half_dim:], -spun[..., :half_dim]], axis=-1)
    return grads * cos_table[:, None, :] + back

def gelu_parts(pre_act):
    normal_cdf = 0.5 * (1.0 + lax.erf(pre_act * (1.0 / math.sqrt(2.0))))
    density = jnp.exp(-0.5 * pre_act * pre_act) * (1.0 / math.sqrt(2.0 * math.pi))
    return (pre_act * normal_cdf, normal_cdf + pre_act * density)

def block_mask(query_ids, key_ids, reach):
    query_count = query_ids.shape[0]
    key_count = key_ids.shape[0]
    distance = jnp.arange(key_count, dtype=jnp.int32)[None, :] - reach - jnp.arange(query_count, dtype=jnp.int32)[:, None]
    return (query_ids[:, None] == key_ids[None, :]) & (jnp.abs(distance) <= reach)

def block_scores(query_rows, key_rows, allowed):
    score_scale = 1.0 / math.sqrt(query_rows.shape[-1])
    scores = jnp.einsum('qhe,khe->hqk', widen(query_rows), widen(key_rows)) * score_scale
    return jnp.where(allowed[None, :, :], scores, MASKED)

def block_forward(query_rows, key_rows, value_rows, allowed):
    scores = block_scores(query_rows, key_rows, allowed)
    row_max = lax.optimization_barrier(jnp.max(scores, axis=-1, keepdims=True))
    log_norm = row_max + jnp.log(lax.optimization_barrier(jnp.sum(jnp.exp(scores - row_max), axis=-1, keepdims=True)))
    attn_probs = to_bf16(jnp.exp(scores - log_norm))
    mixed = to_bf16(jnp.einsum('hqk,khe->qhe', widen(attn_probs), widen(value_rows)))
    return (mixed, log_norm[..., 0])

def block_backward(query_rows, key_rows, value_rows, allowed, log_norm, grad_rows, deltas):
    score_scale = 1.0 / math.sqrt(query_rows.shape[-1])
    scores = block_scores(query_rows, key_rows, allowed)
    probs_full = jnp.exp(scores - log_norm[..., None])
    grad_probs = jnp.einsum('qhe,khe->hqk', widen(grad_rows), widen(value_rows))
    grad_scores = to_bf16(probs_full * (grad_probs - jnp.transpose(deltas)[:, :, None]))
    attn_probs = to_bf16(probs_full)
    grad_queries = jnp.einsum('hqk,khe->qhe', widen(grad_scores), widen(key_rows)) * score_scale
    grad_keys = jnp.einsum('hqk,qhe->khe', widen(grad_scores), widen(query_rows)) * score_scale
    grad_values = jnp.einsum('hqk,qhe->khe', widen(attn_probs), widen(grad_rows))
    return (grad_queries, grad_keys, grad_values)

def attention_forward(queries, keys, values, seq_ids, block_rows, reach):
    total = queries.shape[0]
    span = block_rows + 2 * reach
    keys_pad = jnp.pad(keys, ((reach, reach), (0, 0), (0, 0)))
    values_pad = jnp.pad(values, ((reach, reach), (0, 0), (0, 0)))
    ids_pad = jnp.pad(seq_ids, (reach, reach), constant_values=-1)

    def one_block(block_index):
        first_row = block_index * block_rows
        allowed = block_mask(lax.dynamic_slice_in_dim(seq_ids, first_row, block_rows, 0), lax.dynamic_slice_in_dim(ids_pad, first_row, span, 0), reach)
        return block_forward(lax.dynamic_slice_in_dim(queries, first_row, block_rows, 0), lax.dynamic_slice_in_dim(keys_pad, first_row, span, 0), lax.dynamic_slice_in_dim(values_pad, first_row, span, 0), allowed)
    mixed, log_norm = lax.map(one_block, jnp.arange(total // block_rows, dtype=jnp.int32))
    return (mixed.reshape(total, queries.shape[1], queries.shape[2]), log_norm)

def attention_backward(queries, keys, values, seq_ids, log_norm, grad_mixed, mixed, block_rows, reach):
    total, heads, head_dim = queries.shape
    span = block_rows + 2 * reach
    deltas = lax.optimization_barrier(jnp.sum(widen(grad_mixed) * widen(mixed), axis=-1))
    keys_pad = jnp.pad(keys, ((reach, reach), (0, 0), (0, 0)))
    values_pad = jnp.pad(values, ((reach, reach), (0, 0), (0, 0)))
    ids_pad = jnp.pad(seq_ids, (reach, reach), constant_values=-1)

    def one_step(carry, block_index):
        key_grads, value_grads = carry
        first_row = block_index * block_rows
        allowed = block_mask(lax.dynamic_slice_in_dim(seq_ids, first_row, block_rows, 0), lax.dynamic_slice_in_dim(ids_pad, first_row, span, 0), reach)
        grad_q, grad_k, grad_v = block_backward(lax.dynamic_slice_in_dim(queries, first_row, block_rows, 0), lax.dynamic_slice_in_dim(keys_pad, first_row, span, 0), lax.dynamic_slice_in_dim(values_pad, first_row, span, 0), allowed, log_norm[block_index], lax.dynamic_slice_in_dim(grad_mixed, first_row, block_rows, 0), lax.dynamic_slice_in_dim(deltas, first_row, block_rows, 0))
        key_grads = lax.dynamic_update_slice_in_dim(key_grads, lax.dynamic_slice_in_dim(key_grads, first_row, span, 0) + grad_k, first_row, 0)
        value_grads = lax.dynamic_update_slice_in_dim(value_grads, lax.dynamic_slice_in_dim(value_grads, first_row, span, 0) + grad_v, first_row, 0)
        return ((key_grads, value_grads), grad_q)
    zero_pad = jnp.zeros((total + 2 * reach, heads, head_dim), jnp.float32)
    (key_grads, value_grads), query_grads = lax.scan(one_step, (zero_pad, zero_pad), jnp.arange(total // block_rows, dtype=jnp.int32))
    return (query_grads.reshape(total, heads, head_dim), key_grads[reach:reach + total], value_grads[reach:reach + total])

def adam_update(weight, moments, grad, decay):
    first_moment = BETA_ONE * moments[0] + (1.0 - BETA_ONE) * grad
    second_moment = BETA_TWO * moments[1] + (1.0 - BETA_TWO) * grad * grad
    first_hat = first_moment / (1.0 - BETA_ONE ** STEP)
    second_hat = second_moment / (1.0 - BETA_TWO ** STEP)
    new_weight = weight - LEARN_RATE * (first_hat / (jnp.sqrt(second_hat) + ADAM_EPS) + decay * weight)
    return (new_weight, jnp.stack([first_moment, second_moment]))

def reference(residual_in, out_cotangent, seq_lengths, qkv_weight, out_weight, in_weight, down_weight, norm_gains, qkv_moments, out_moments, in_moments, down_moments, gain_moments):
    total = residual_in.shape[0]
    block_rows = min(512, TOK_DEV)
    reach = HALF_WIN
    places = jnp.arange(total, dtype=jnp.int32)
    seq_ids, offsets = seq_coords(seq_lengths, places)
    cos_table, sin_table = rotary_tables(offsets, HD)
    qkv_bf = to_bf16(qkv_weight)
    out_bf = to_bf16(out_weight)
    in_flat = to_bf16(in_weight).reshape(D, 2 * FF)
    down_bf = to_bf16(down_weight)
    first_normed, first_inv, first_scaled = norm_forward(residual_in, norm_gains[0])
    normed_in = to_bf16(first_scaled)
    proj = matmul(normed_in, qkv_bf).reshape(total, H, 3, HD)
    queries = to_bf16(rotate(proj[:, :, 0], cos_table, sin_table))
    keys = to_bf16(rotate(proj[:, :, 1], cos_table, sin_table))
    values = to_bf16(proj[:, :, 2])
    mixed, log_norm = attention_forward(queries, keys, values, seq_ids, block_rows, reach)
    mixed_flat = mixed.reshape(total, D)
    middle = residual_in + matmul(mixed_flat, out_bf)
    second_normed, second_inv, second_scaled = norm_forward(middle, norm_gains[1])
    ffn_in = to_bf16(second_scaled)
    both = matmul(ffn_in, in_flat).reshape(total, 2, FF)
    activated, slope = gelu_parts(both[:, 0])
    gated = to_bf16(activated * both[:, 1])
    block_out = middle + matmul(gated, down_bf)
    out_grad_bf = to_bf16(out_cotangent)
    down_grad = matmul(gated.T, out_grad_bf)
    grad_gated = matmul(out_grad_bf, down_bf.T)
    grad_both = to_bf16(jnp.stack([grad_gated * both[:, 1] * slope, grad_gated * activated], axis=1))
    grad_both_flat = grad_both.reshape(total, 2 * FF)
    in_grad = matmul(ffn_in.T, grad_both_flat).reshape(D, 2, FF)
    grad_ffn_in = matmul(grad_both_flat, in_flat.T)
    grad_second, second_gain_grad = norm_backward(grad_ffn_in, second_normed, second_inv, norm_gains[1])
    grad_middle = out_cotangent + grad_second
    middle_bf = to_bf16(grad_middle)
    out_weight_grad = matmul(mixed_flat.T, middle_bf)
    grad_mixed = to_bf16(matmul(middle_bf, out_bf.T)).reshape(total, H, HD)
    grad_queries, grad_keys, grad_values = attention_backward(queries, keys, values, seq_ids, log_norm, grad_mixed, mixed, block_rows, reach)
    grad_proj = to_bf16(jnp.stack([unrotate(grad_queries, cos_table, sin_table), unrotate(grad_keys, cos_table, sin_table), grad_values], axis=2))
    grad_proj_flat = grad_proj.reshape(total, 3 * D)
    qkv_grad = matmul(normed_in.T, grad_proj_flat)
    grad_first, first_gain_grad = norm_backward(matmul(grad_proj_flat, qkv_bf.T), first_normed, first_inv, norm_gains[0])
    residual_grad = grad_middle + grad_first
    gains_grad = jnp.stack([first_gain_grad, second_gain_grad])
    new_qkv, new_qkv_moments = adam_update(qkv_weight, qkv_moments, qkv_grad, DECAY_RATE)
    new_out, new_out_moments = adam_update(out_weight, out_moments, out_weight_grad, DECAY_RATE)
    new_in, new_in_moments = adam_update(in_weight, in_moments, in_grad, DECAY_RATE)
    new_down, new_down_moments = adam_update(down_weight, down_moments, down_grad, DECAY_RATE)
    new_gains, new_gain_moments = adam_update(norm_gains, gain_moments, gains_grad, 0.0)
    return (block_out, residual_grad, qkv_grad, out_weight_grad, in_grad, down_grad, gains_grad, new_qkv, new_out, new_in, new_down, new_gains, new_qkv_moments, new_out_moments, new_in_moments, new_down_moments, new_gain_moments)
```

```python
import functools
import math

import jax
import jax.numpy as jnp
from jax import lax
from jax.experimental import pallas as pl
from jax.experimental.pallas import tpu as pltpu
from jax.sharding import PartitionSpec as P

HD = 64
HALF_WIN = 64
STEP = 3


NORM_EPS = 1e-05
ROPE_BASE = 10000.0
BETA_ONE = 0.9
BETA_TWO = 0.999
ADAM_EPS = 1e-08
LEARN_RATE = 0.005
DECAY_RATE = 0.1
MASKED = -1e30

MESH = pl.DeviceIdType.MESH
DEPTH, SIDES, CORES = 4, 2, 2
DIRECT = 3


def gather_kernel(count, *refs):
    shards, fulls = refs[:count], refs[count : 2 * count]
    own_sem, z_send, z_recv, y_send, y_recv, c_send, c_recv = refs[2 * count :]
    me = lax.axis_index("dp")
    z, y, c = me // 4, (me // 2) % 2, me % 2
    z_peers = [lax.rem(z + d, DEPTH) * 4 + y * 2 + c for d in range(1, DEPTH)]
    y_peer = z * 4 + (1 - y) * 2 + c
    c_peer = z * 4 + y * 2 + (1 - c)

    barrier = pltpu.get_barrier_semaphore()
    for peer in z_peers + [y_peer, c_peer]:
        pl.semaphore_signal(barrier, inc=1, device_id={"dp": peer}, device_id_type=MESH)
    pl.semaphore_wait(barrier, DEPTH + 1)

    def block(i, d, side):
        rows = shards[i].shape[0]
        origin = lax.rem(z - d + DEPTH, DEPTH) * 4 + (y if side == 0 else 1 - y) * 2 + c
        return fulls[i].at[pl.ds(pl.multiple_of(origin * rows, rows), rows), :]

    def send(src, dst, sem_s, sem_r, peer):
        copy = pltpu.make_async_remote_copy(
            src_ref=src,
            dst_ref=dst,
            send_sem=sem_s,
            recv_sem=sem_r,
            device_id={"dp": peer},
            device_id_type=MESH,
        )
        copy.start()
        return copy

    own, z_copies, y_copies, c_copies = [], {}, {}, {}
    for i in range(count):
        own.append(pltpu.make_async_copy(shards[i], block(i, 0, 0), own_sem.at[i]))
        own[-1].start()
        for d in range(1, DEPTH):
            z_copies[i, d] = send(
                shards[i], block(i, 0, 0), z_send.at[i, d - 1], z_recv.at[i, d - 1], z_peers[d - 1]
            )
        y_copies[i, 0] = send(shards[i], block(i, 0, 0), y_send.at[i, 0], y_recv.at[i, 0], y_peer)
        c_copies[i, 0] = send(shards[i], block(i, 0, 0), c_send.at[i, 0], c_recv.at[i, 0], c_peer)
    for i in range(count):
        for d in range(1, DEPTH):
            z_copies[i, d].wait_recv()
            here = block(i, d, 0)
            y_copies[i, d] = send(here, here, y_send.at[i, d], y_recv.at[i, d], y_peer)
            c_copies[i, 2 * d] = send(here, here, c_send.at[i, 2 * d], c_recv.at[i, 2 * d], c_peer)
    for i in range(count):
        for d in range(DEPTH):
            y_copies[i, d].wait_recv()
            here = block(i, d, 1)
            k = 2 * d + 1
            c_copies[i, k] = send(here, here, c_send.at[i, k], c_recv.at[i, k], c_peer)
    for i in range(count):
        for k in range(2 * DEPTH):
            c_copies[i, k].wait_recv()
    for copy in own:
        copy.wait()
    for table in (z_copies, y_copies, c_copies):
        for copy in table.values():
            copy.wait_send()


def gather_all(*shards):
    count = len(shards)
    total = sum(math.prod(s.shape) for s in shards) * 2
    return pl.pallas_call(
        functools.partial(gather_kernel, count),
        out_shape=[
            jax.ShapeDtypeStruct((s.shape[0] * DEPTH * SIDES * CORES, s.shape[1]), s.dtype)
            for s in shards
        ],
        in_specs=[pl.BlockSpec(memory_space=pltpu.VMEM)] * count,
        out_specs=[pl.BlockSpec(memory_space=pl.ANY)] * count,
        scratch_shapes=[
            pltpu.SemaphoreType.DMA((count,)),
            pltpu.SemaphoreType.DMA((count, 3)),
            pltpu.SemaphoreType.DMA((count, 3)),
            pltpu.SemaphoreType.DMA((count, 4)),
            pltpu.SemaphoreType.DMA((count, 4)),
            pltpu.SemaphoreType.DMA((count, 8)),
            pltpu.SemaphoreType.DMA((count, 8)),
        ],
        compiler_params=pltpu.CompilerParams(
            collective_id=1, has_side_effects=True, vmem_limit_bytes=8 << 20
        ),
        cost_estimate=pl.CostEstimate(flops=0, bytes_accessed=total * 200, transcendentals=0),
    )(*shards)


def sum_everywhere(value):
    for axis in ("tensor", "dp"):
        size, step = lax.axis_size(axis), 1
        if size & (size - 1):
            value = lax.psum(value, axis)
            continue
        while step < size:
            value = value + lax.ppermute(value, axis, [(i, i ^ step) for i in range(size)])
            step *= 2
    return value


def gather_tokens(value):
    size = lax.axis_size("tensor")
    if size != 2:
        return lax.all_gather(value, "tensor", axis=0, tiled=True)
    rows = value.shape[0]
    index = lax.axis_index("tensor")
    other = lax.ppermute(value, "tensor", [(0, 1), (1, 0)])
    whole = jnp.zeros((2 * rows,) + value.shape[1:], value.dtype)
    whole = lax.dynamic_update_slice_in_dim(whole, value, index * rows, 0)
    return lax.dynamic_update_slice_in_dim(whole, other, (1 - index) * rows, 0)


def scatter_tokens(left, multiply):
    size = lax.axis_size("tensor")
    if size != 2:
        part = multiply(left).astype(jnp.bfloat16)
        return lax.psum_scatter(part, "tensor", scatter_dimension=0, tiled=True).astype(
            jnp.float32
        )
    rows = left.shape[0] // 2
    index = lax.axis_index("tensor")
    theirs = lax.dynamic_slice_in_dim(left, (1 - index) * rows, rows, 0)
    ours = lax.dynamic_slice_in_dim(left, index * rows, rows, 0)
    sent = multiply(theirs).astype(jnp.bfloat16)
    got = lax.ppermute(sent, "tensor", [(0, 1), (1, 0)])
    return multiply(ours) + got.astype(jnp.float32)


def padded(value, sides, width):
    for axis, dim in sides:
        size, length = (lax.axis_size(axis), value.shape[dim])
        up = [(i, (i + 1) % size) for i in range(size - 1)]
        down = [(j, i) for i, j in up]
        last = lax.slice_in_dim(value, length - width, length, axis=dim)
        first = lax.slice_in_dim(value, 0, width, axis=dim)
        before = lax.ppermute(last, axis, up)
        after = lax.ppermute(first, axis, down)
        value = jnp.concatenate([before, value, after], axis=dim)
    return value


def norm_forward(rows, gain):
    row_mean = jnp.mean(rows, axis=-1, keepdims=True)
    centered = rows - row_mean
    inv_std = lax.rsqrt(jnp.mean(centered * centered, axis=-1, keepdims=True) + NORM_EPS)
    normed = centered * inv_std
    return (normed, inv_std, normed * gain)


def norm_backward(grad_out, normed, inv_std, gain):
    scaled = grad_out * gain
    grad_rows = inv_std * (
        scaled
        - jnp.mean(scaled, axis=-1, keepdims=True)
        - normed * jnp.mean(scaled * normed, axis=-1, keepdims=True)
    )
    return (grad_rows, jnp.sum(grad_out * normed, axis=0))


def seq_coords(seq_lengths, places):
    seq_ends = jnp.cumsum(seq_lengths, dtype=jnp.int32)
    passed = (seq_ends[None, :] <= places[:, None]).astype(jnp.int32)
    seq_ids = jnp.sum(passed, axis=1, dtype=jnp.int32)
    seq_start = jnp.sum(passed * seq_lengths[None, :], axis=1, dtype=jnp.int32)
    return (seq_ids, places - seq_start)


def rotary_tables(offsets, head_dim):
    half_dim = head_dim // 2
    inv_freq = ROPE_BASE ** (-2.0 * jnp.arange(half_dim).astype(jnp.float32) / head_dim)
    angles = offsets.astype(jnp.float32)[:, None] * inv_freq[None, :]
    cos_table = jnp.cos(angles)
    sin_table = jnp.sin(angles)
    return (
        jnp.concatenate([cos_table, cos_table], axis=-1),
        jnp.concatenate([sin_table, sin_table], axis=-1),
    )


def rotate(feats, cos_table, sin_table):
    half_dim = feats.shape[-1] // 2
    turned = jnp.concatenate([-feats[..., half_dim:], feats[..., :half_dim]], axis=-1)
    return feats * cos_table[:, None, :] + turned * sin_table[:, None, :]


def unrotate(grads, cos_table, sin_table):
    half_dim = grads.shape[-1] // 2
    spun = grads * sin_table[:, None, :]
    back = jnp.concatenate([spun[..., half_dim:], -spun[..., :half_dim]], axis=-1)
    return grads * cos_table[:, None, :] + back


def gelu_parts(pre_act):
    normal_cdf = 0.5 * (1.0 + lax.erf(pre_act * (1.0 / math.sqrt(2.0))))
    density = jnp.exp(-0.5 * pre_act * pre_act) * (1.0 / math.sqrt(2.0 * math.pi))
    return (pre_act * normal_cdf, normal_cdf + pre_act * density)


def block_mask(query_ids, key_ids, reach):
    query_count = query_ids.shape[0]
    key_count = key_ids.shape[0]
    distance = (
        jnp.arange(key_count, dtype=jnp.int32)[None, :]
        - reach
        - jnp.arange(query_count, dtype=jnp.int32)[:, None]
    )
    return (query_ids[:, None] == key_ids[None, :]) & (jnp.abs(distance) <= reach)


def block_scores(query_rows, key_rows, allowed):
    score_scale = 1.0 / math.sqrt(query_rows.shape[-1])
    scores = (
        jnp.einsum("qhe,khe->hqk", query_rows, key_rows, preferred_element_type=jnp.float32)
        * score_scale
    )
    return jnp.where(allowed[None, :, :], scores, MASKED)


def block_forward(query_rows, key_rows, value_rows, allowed):
    scores = block_scores(query_rows, key_rows, allowed)
    row_max = jnp.max(scores, axis=-1, keepdims=True)
    log_norm = row_max + jnp.log(jnp.sum(jnp.exp(scores - row_max), axis=-1, keepdims=True))
    attn_probs = jnp.exp(scores - log_norm).astype(jnp.bfloat16)
    mixed = jnp.einsum("hqk,khe->qhe", attn_probs, value_rows, preferred_element_type=jnp.float32)
    return (mixed.astype(jnp.bfloat16), log_norm[..., 0])


def block_backward(query_rows, key_rows, value_rows, allowed, log_norm, grad_rows, deltas):
    score_scale = 1.0 / math.sqrt(query_rows.shape[-1])
    scores = block_scores(query_rows, key_rows, allowed)
    probs_full = jnp.exp(scores - log_norm[..., None])
    grad_probs = jnp.einsum(
        "qhe,khe->hqk", grad_rows, value_rows, preferred_element_type=jnp.float32
    )
    grad_scores = (probs_full * (grad_probs - jnp.transpose(deltas)[:, :, None])).astype(
        jnp.bfloat16
    )
    attn_probs = probs_full.astype(jnp.bfloat16)
    grad_queries = (
        jnp.einsum("hqk,khe->qhe", grad_scores, key_rows, preferred_element_type=jnp.float32)
        * score_scale
    )
    grad_keys = (
        jnp.einsum("hqk,qhe->khe", grad_scores, query_rows, preferred_element_type=jnp.float32)
        * score_scale
    )
    grad_values = jnp.einsum(
        "hqk,qhe->khe", attn_probs, grad_rows, preferred_element_type=jnp.float32
    )
    return (grad_queries, grad_keys, grad_values)


def product_rows(matrix, weight, contract_dim):
    return lax.dot_general(
        matrix, weight, (((1,), (contract_dim,)), ((), ())), preferred_element_type=jnp.float32
    )


def across_rows(left, right):
    return lax.dot_general(
        left, right, (((0,), (0,)), ((), ())), preferred_element_type=jnp.float32
    )


def against_cols(left, right):
    return lax.dot_general(
        left, right, (((1,), (1,)), ((), ())), preferred_element_type=jnp.float32
    )


def adam_update(weight, moments, grad, decay):
    first_moment = BETA_ONE * moments[0] + (1.0 - BETA_ONE) * grad
    second_moment = BETA_TWO * moments[1] + (1.0 - BETA_TWO) * grad * grad
    first_hat = first_moment / (1.0 - BETA_ONE**STEP)
    second_hat = second_moment / (1.0 - BETA_TWO**STEP)
    new_weight = weight - LEARN_RATE * (
        first_hat / (jnp.sqrt(second_hat) + ADAM_EPS) + decay * weight
    )
    return (new_weight, jnp.stack([first_moment, second_moment]))


def local(
    residual_in,
    out_cotangent,
    seq_lengths,
    qkv_weight,
    out_weight,
    in_weight,
    down_weight,
    norm_gains,
    qkv_moments,
    out_moments,
    in_moments,
    down_moments,
    gain_moments,
):
    tensor_count = lax.axis_size("tensor")
    data_count = lax.axis_size("dp")
    local_rows = residual_in.shape[0]
    seq_rows = local_rows * tensor_count
    reach = HALF_WIN
    block_rows = min(512, seq_rows)
    span = block_rows + 2 * reach
    cast = lambda w: w.astype(jnp.bfloat16)
    shards = [
        cast(qkv_weight),
        cast(out_weight).T,
        cast(in_weight[:, 0]),
        cast(in_weight[:, 1]),
        cast(down_weight).T,
    ]
    grad_out_all = gather_tokens(out_cotangent.astype(jnp.bfloat16))
    first_normed, first_inv, first_scaled = norm_forward(residual_in, norm_gains[0])
    normed_in = gather_tokens(first_scaled.astype(jnp.bfloat16))
    direct = DIRECT if (data_count, tensor_count) == (16, 2) else 0
    fulls = list(gather_all(*shards[:direct])) if direct else []
    fulls += [lax.all_gather(w, "dp", axis=0, tiled=True) for w in shards[direct:]]
    qkv_full, out_full, act_full, gate_full, down_full = fulls
    model_dim = qkv_full.shape[0]
    head_dim = HD
    local_heads = qkv_full.shape[1] // (3 * head_dim)
    head_feats = local_heads * head_dim
    first_token = lax.axis_index("dp") * seq_rows
    places = first_token + jnp.arange(seq_rows, dtype=jnp.int32)
    query_ids, offsets = seq_coords(seq_lengths, places)
    cos_table, sin_table = rotary_tables(offsets, head_dim)
    key_places = first_token - reach + jnp.arange(seq_rows + 2 * reach, dtype=jnp.int32)
    inside = (key_places >= 0) & (key_places < seq_rows * data_count)
    key_ids = jnp.where(inside, seq_coords(seq_lengths, key_places)[0], -1)
    proj = jnp.dot(normed_in, qkv_full, preferred_element_type=jnp.float32).reshape(
        seq_rows, local_heads, 3, head_dim
    )
    queries = rotate(proj[:, :, 0], cos_table, sin_table).astype(jnp.bfloat16)
    keys = rotate(proj[:, :, 1], cos_table, sin_table).astype(jnp.bfloat16)
    values = proj[:, :, 2].astype(jnp.bfloat16)
    key_vals = jnp.concatenate(
        [keys.reshape(seq_rows, head_feats), values.reshape(seq_rows, head_feats)], axis=1
    )
    key_vals_pad = padded(key_vals, (("dp", 0),), reach)
    keys_pad = key_vals_pad[:, :head_feats].reshape(seq_rows + 2 * reach, local_heads, head_dim)
    values_pad = key_vals_pad[:, head_feats:].reshape(seq_rows + 2 * reach, local_heads, head_dim)
    allowed = block_mask(query_ids, key_ids, reach)
    mixed_part, norm_part = block_forward(queries, keys_pad, values_pad, allowed)
    mixed_flat = mixed_part.reshape(seq_rows, head_feats)
    attn_out = scatter_tokens(mixed_flat, lambda r: against_cols(r, out_full))
    middle = residual_in + attn_out
    second_normed, second_inv, second_scaled = norm_forward(middle, norm_gains[1])
    ffn_in = gather_tokens(second_scaled.astype(jnp.bfloat16))
    act_pre = jnp.dot(ffn_in, act_full, preferred_element_type=jnp.float32)
    gate = jnp.dot(ffn_in, gate_full, preferred_element_type=jnp.float32)
    activated, slope = gelu_parts(act_pre)
    gated = (activated * gate).astype(jnp.bfloat16)
    grad_gated = jnp.dot(grad_out_all, down_full, preferred_element_type=jnp.float32)
    grad_act = (grad_gated * gate * slope).astype(jnp.bfloat16)
    grad_gate = (grad_gated * activated).astype(jnp.bfloat16)
    if tensor_count == 2:
        own = lax.axis_index("tensor")
        near = lambda v, at: lax.dynamic_slice_in_dim(v, at * local_rows, local_rows, 0)
        back = lambda at: against_cols(near(grad_act, at), act_full) + against_cols(
            near(grad_gate, at), gate_full
        )
        sent = back(1 - own).astype(jnp.bfloat16)
        got = lax.ppermute(sent, "tensor", [(0, 1), (1, 0)])
        grad_ffn_in = back(own) + got.astype(jnp.float32)
    else:
        grad_ffn_in = lax.psum_scatter(
            (against_cols(grad_act, act_full) + against_cols(grad_gate, gate_full)).astype(
                jnp.bfloat16
            ), "tensor", scatter_dimension=0, tiled=True
        ).astype(jnp.float32)
    ffn_parts = jnp.concatenate(
        [
            across_rows(grad_out_all, gated).astype(jnp.bfloat16),
            across_rows(ffn_in, grad_act).astype(jnp.bfloat16),
            across_rows(ffn_in, grad_gate).astype(jnp.bfloat16),
        ],
        axis=1,
    )
    grad_ffn_in, ffn_parts = lax.optimization_barrier((grad_ffn_in, ffn_parts))
    ffn_grads = lax.psum_scatter(ffn_parts, "dp", scatter_dimension=0, tiled=True).astype(
        jnp.float32
    )
    ffn_out = scatter_tokens(gated, lambda r: against_cols(r, down_full))
    block_out = middle + ffn_out
    grad_second, second_gain_part = norm_backward(
        grad_ffn_in, second_normed, second_inv, norm_gains[1]
    )
    grad_middle = out_cotangent + grad_second
    middle_all = gather_tokens(grad_middle.astype(jnp.bfloat16))
    out_grad_part = across_rows(middle_all, mixed_flat).astype(jnp.bfloat16)
    grad_mixed = (
        jnp.dot(middle_all, out_full, preferred_element_type=jnp.float32)
        .astype(jnp.bfloat16)
        .reshape(seq_rows, local_heads, head_dim)
    )
    deltas = jnp.sum(grad_mixed.astype(jnp.float32) * mixed_part.astype(jnp.float32), axis=-1)
    grad_kv_pad = jnp.zeros((seq_rows + 2 * reach, 2 * head_feats), jnp.float32)
    allowed = block_mask(query_ids, key_ids, reach)
    grad_q, grad_k, grad_v = block_backward(
        queries, keys_pad, values_pad, allowed, norm_part, grad_mixed, deltas
    )
    update = jnp.concatenate(
        [grad_k.reshape(span, head_feats), grad_v.reshape(span, head_feats)], axis=1
    )
    grad_kv_pad = grad_kv_pad.at[0:span].add(update)
    edge_grads = jnp.concatenate([grad_kv_pad[:reach], grad_kv_pad[seq_rows + reach :]], axis=0)
    edge_ext = padded(edge_grads.astype(jnp.bfloat16), (("dp", 0),), reach).astype(edge_grads.dtype)
    own_grads = grad_kv_pad[reach : reach + seq_rows]
    own_grads = own_grads.at[:reach].add(edge_ext[:reach])
    own_grads = own_grads.at[seq_rows - reach :].add(edge_ext[3 * reach :])
    grad_keys = own_grads[:, :head_feats].reshape(seq_rows, local_heads, head_dim)
    grad_values = own_grads[:, head_feats:].reshape(seq_rows, local_heads, head_dim)
    grad_proj = jnp.stack(
        [
            unrotate(grad_q, cos_table, sin_table),
            unrotate(grad_keys, cos_table, sin_table),
            grad_values,
        ],
        axis=2,
    )
    grad_proj_flat = grad_proj.astype(jnp.bfloat16).reshape(seq_rows, 3 * head_feats)
    qkv_grad_part = across_rows(normed_in, grad_proj_flat)
    attn_parts = jnp.concatenate([qkv_grad_part.astype(jnp.bfloat16), out_grad_part], axis=1)
    attn_parts, ffn_grads = lax.optimization_barrier((attn_parts, ffn_grads))
    hidden = gated.shape[1]
    down_grad = ffn_grads[:, :hidden].T
    in_grad = jnp.stack([ffn_grads[:, hidden : 2 * hidden], ffn_grads[:, 2 * hidden :]], axis=1)
    attn_grads = lax.psum_scatter(attn_parts, "dp", scatter_dimension=0, tiled=True).astype(
        jnp.float32
    )
    qkv_grad = attn_grads[:, : 3 * head_feats]
    out_weight_grad = attn_grads[:, 3 * head_feats :].T
    grad_norm_in = scatter_tokens(grad_proj_flat, lambda r: against_cols(r, qkv_full))
    grad_first, first_gain_part = norm_backward(
        grad_norm_in, first_normed, first_inv, norm_gains[0]
    )
    residual_grad = grad_middle + grad_first
    gains_grad = sum_everywhere(jnp.stack([first_gain_part, second_gain_part]))
    new_qkv, new_qkv_moments = adam_update(qkv_weight, qkv_moments, qkv_grad, DECAY_RATE)
    new_out, new_out_moments = adam_update(out_weight, out_moments, out_weight_grad, DECAY_RATE)
    new_in, new_in_moments = adam_update(in_weight, in_moments, in_grad, DECAY_RATE)
    new_down, new_down_moments = adam_update(down_weight, down_moments, down_grad, DECAY_RATE)
    new_gains, new_gain_moments = adam_update(norm_gains, gain_moments, gains_grad, 0.0)
    return (
        block_out,
        residual_grad,
        qkv_grad,
        out_weight_grad,
        in_grad,
        down_grad,
        gains_grad,
        new_qkv,
        new_out,
        new_in,
        new_down,
        new_gains,
        new_qkv_moments,
        new_out_moments,
        new_in_moments,
        new_down_moments,
        new_gain_moments,
    )


def solution(mesh):
    return jax.shard_map(
        local,
        mesh=mesh,
        in_specs=(
            P(("dp", "tensor"), None),
            P(("dp", "tensor"), None),
            P(),
            P("dp", "tensor"),
            P("tensor", "dp"),
            P("dp", None, "tensor"),
            P("tensor", "dp"),
            P(),
            P(None, "dp", "tensor"),
            P(None, "tensor", "dp"),
            P(None, "dp", None, "tensor"),
            P(None, "tensor", "dp"),
            P(),
        ),
        out_specs=(
            P(("dp", "tensor"), None),
            P(("dp", "tensor"), None),
            P("dp", "tensor"),
            P("tensor", "dp"),
            P("dp", None, "tensor"),
            P("tensor", "dp"),
            P(),
            P("dp", "tensor"),
            P("tensor", "dp"),
            P("dp", None, "tensor"),
            P("tensor", "dp"),
            P(),
            P(None, "dp", "tensor"),
            P(None, "tensor", "dp"),
            P(None, "dp", None, "tensor"),
            P(None, "tensor", "dp"),
            P(),
        ),
        check_vma=False,
    )
```
